32 devices in a mesh: grp: 2 (over y), tm: 4 (over z), tmpl: 4 (over x, core).
Axes of the slice: x: 2, y: 2, z: 4, core: 2. Of those that a mesh axis runs over, the one named last changes fastest.
Arguments:
- records: bfloat16 [160, 3072], P(None, ('grp', 'tm')), parts along dimension 1, may hold values from -600 to 600
- templates: bfloat16 [160, 4, 4, 200], P(None, 'tm', 'tmpl'), may hold values from -60 to 60
- channel_mask: int32 [160, 4, 4], P(None, 'tm', 'tmpl'), may hold values 0 or 1
- lag_table: int32 [160, 4, 4], P(None, 'tm', 'tmpl'), may hold values from 0 to 63
Outputs:
- stacked: float32 [4, 4, 3072], P(None, 'tmpl', ('grp', 'tm')), parts along dimension 2
The draws below stay inside these ranges and needn't reach their ends.
There are 2 independent parts, one for each index of `grp`. The reference program is written for one: setup_inputs(seed, part) draws one part's arguments, and reference() takes and returns one part's arrays. A program takes and returns all parts, laid end to end along the dimension named above; an argument that names none is the same for every part. Nothing has to cross between parts.
All inputs are finite; a program needn't handle non-finite values. No bound on the sum of `channel_mask` on one device may be relied on, other than what follows from the above.
Results may differ from the reference program's by a relative error of at most 0.0003.
Values may be sent and summed in bfloat16 or wider, within the bound.
A program may use at most 192 MiB of HBM per device.

```python
import math
import jax
import jax.numpy as jnp
from jax import lax

C = 160
L = 200
LAGS = 64
NT = 1536
KA = 4
KB = 4


def draw_records(key, part):
    key_base, key_chan, key_seg = jax.random.split(key, 3)
    base_noise = jnp.clip(jax.random.normal(key_base, (C, NT), jnp.float32), -6.0, 6.0)
    log_reach = math.log(10.0)
    channel_gain = jnp.exp(jax.random.uniform(key_chan, (C, 1), jnp.float32, 0.0, log_reach))
    segment_gain = jnp.exp(jax.random.uniform(key_seg, (C, NT // 32, 1), jnp.float32, 0.0, log_reach))
    values = (base_noise.reshape(C, NT // 32, 32) * segment_gain).reshape(C, NT) * channel_gain
    return values.astype(jnp.bfloat16)


def draw_templates(key, part):
    key_base, key_gain = jax.random.split(jax.random.fold_in(key, 7), 2)
    base_noise = jnp.clip(jax.random.normal(key_base, (C, KA, KB, L), jnp.float32), -6.0, 6.0)
    log_reach = math.log(10.0)
    channel_gain = jnp.exp(jax.random.uniform(key_gain, (C, KA, KB, 1), jnp.float32, 0.0, log_reach))
    return (base_noise * channel_gain).astype(jnp.bfloat16)


def place_ends(values, rng, low, largest):
    dims = values.shape
    spot = [jax.random.randint(jax.random.fold_in(rng, axis), (), 0, dims[axis]) for axis in range(len(dims))]
    values = values.at[tuple(spot)].set(low)
    longest = dims.index(max(dims))
    spot[longest] = (spot[longest] + 1) % dims[longest]
    return values.at[tuple(spot)].set(largest)


def setup_inputs(seed: int = 0, part: int = 0) -> dict:
    streams_of = jax.random.split(jax.random.key(seed), 5)
    part_keys = jax.random.split(jax.random.fold_in(streams_of[4], part), 5)
    return {
        "records": draw_records(jax.random.fold_in(jax.random.fold_in(streams_of[4], part), 71), part),
        "templates": draw_templates(jax.random.fold_in(streams_of[4], 71), part),
        "channel_mask": place_ends((jax.random.randint(streams_of[2], (C, KA, KB), 0, 4) < 3).astype(jnp.int32), jax.random.fold_in(streams_of[2], 1), 0, 1),
        "lag_table": place_ends(jax.random.randint(streams_of[3], (C, KA, KB), 0, LAGS), jax.random.fold_in(streams_of[3], 1), 0, LAGS - 1).astype(jnp.int32),
    }


def energy_scale(extended):
    squares = jnp.square(extended.astype(jnp.float32))
    window = lax.reduce_window(squares, jnp.zeros((), squares.dtype), lax.add, (1, L), (1, 1), 'VALID')
    return lax.rsqrt(window / L + 1e-05)

def stack_part(extended, inverse_rms, kernels, in_use, lag_rows, out_len):
    channels, template_count, tmpl_len = kernels.shape
    kernel_flat = kernels.reshape(channels * template_count, 1, tmpl_len)
    products = lax.conv_general_dilated(extended[None], kernel_flat, (1,), 'VALID', dimension_numbers=('NCH', 'OIH', 'NCH'), feature_group_count=channels, preferred_element_type=jnp.float32)[0]
    products = products.reshape(channels, template_count, -1)
    normalized = products * inverse_rms[:, None, :]
    positions = lag_rows.astype(jnp.int32)[:, :, None] + jnp.arange(out_len, dtype=jnp.int32)[None, None, :]
    aligned = jnp.take_along_axis(normalized, positions, axis=2)
    as_float = kernels.astype(jnp.float32)
    kernel_rms = jnp.sqrt(lax.optimization_barrier(jnp.mean(as_float * as_float, axis=2)) + 1e-05)
    weight = in_use.astype(jnp.float32) / (kernel_rms * tmpl_len)
    return jnp.einsum('cnt,cn->nt', aligned, weight, precision=lax.Precision.HIGHEST)

def reference(records, templates, channel_mask, lag_table):
    channels, record_len = records.shape
    extended = jnp.concatenate([records, jnp.zeros((channels, L + LAGS - 1), records.dtype)], axis=1)
    inverse_rms = energy_scale(extended)
    kernel_rows = jnp.moveaxis(templates, 1, 0)
    mask_rows = jnp.moveaxis(channel_mask, 1, 0)
    lag_rows = jnp.moveaxis(lag_table, 1, 0)

    def one_template_row(members):
        kernels, in_use, lags_here = members
        return stack_part(extended, inverse_rms, kernels, in_use, lags_here, record_len)
    return lax.map(one_template_row, (kernel_rows, mask_rows, lag_rows))
```

```python
import functools

import jax
import jax.numpy as jnp
from jax import lax
from jax.experimental import pallas as pl
from jax.experimental.pallas import tpu as pltpu
from jax.sharding import PartitionSpec as P

LAGS = 64
LANES = 128
STEP = 32
ROWS = 16


def up(value, unit):
    return -(-value // unit) * unit


def shifted_left(values, count):
    width = values.shape[1]
    if count % width == 0:
        return values
    return pltpu.roll(values, width - count % width, 1)


def window_sum(values, length):
    total, done, power, span = None, 0, values, 1
    while True:
        if length & span:
            part = shifted_left(power, done)
            total = part if total is None else total + part
            done += span
        if span * 2 > length:
            return total
        power = power + shifted_left(power, span)
        span *= 2


def correlate(tmpl_len, count, ext_ref, tmpl_ref, code_ref, out_ref, wide_ref, trace_ref, spread_ref):
    channels, ext_len = ext_ref.shape
    slab_len = out_ref.shape[1]
    tmpl_pad = tmpl_ref.shape[2]
    span = trace_ref.shape[2]
    blocks = -(-tmpl_len // STEP)
    wide = blocks * STEP * ROWS
    deep = STEP * ROWS
    reach = up(slab_len + LAGS - 1 + (blocks - 1) * STEP, LANES)

    lane = lax.broadcasted_iota(jnp.int32, (tmpl_pad, wide), 1)
    sample = lax.broadcasted_iota(jnp.int32, (tmpl_pad, wide), 0)
    spread_ref[...] = jnp.where(lane // ROWS == sample, 1.0, 0.0).astype(jnp.bfloat16)
    own = lax.broadcasted_iota(jnp.int32, (channels, wide), 1) % ROWS == (
        lax.broadcasted_iota(jnp.int32, (channels, wide), 0) % ROWS
    )
    for n in range(count):
        widened = jnp.dot(tmpl_ref[n], spread_ref[...], preferred_element_type=jnp.float32)
        wide_ref[n] = jnp.where(own, widened, 0.0).astype(jnp.bfloat16)

    @pl.loop(0, channels // ROWS)
    def _(group):
        rows = pl.ds(pl.multiple_of(group * ROWS, ROWS), ROWS)
        series = ext_ref[rows, :]
        as_float = series.astype(jnp.float32)
        energy = window_sum(as_float * as_float, tmpl_len)[:, :span]
        inverse_rms = lax.rsqrt(energy / tmpl_len + 1e-05)
        moved = jnp.concatenate(
            [shifted_left(as_float, b)[:, :reach].astype(jnp.bfloat16) for b in range(STEP)], axis=0
        )
        for n in range(count):
            left = jnp.concatenate(
                [wide_ref[n, rows, a * deep : (a + 1) * deep] for a in range(blocks)], axis=0
            )
            partial = jnp.dot(left, moved, preferred_element_type=jnp.float32)
            per_tile = LANES // STEP
            total = None
            for phase in range(min(per_tile, blocks)):
                lined = None
                for a in range(phase, blocks, per_tile):
                    start = (a - phase) * STEP
                    piece = partial[a * ROWS : (a + 1) * ROWS, start:]
                    piece = piece[:, : min(span + LANES, reach - start)]
                    if piece.shape[1] < span + LANES:
                        piece = jnp.concatenate(
                            [piece, jnp.zeros((ROWS, span + LANES - piece.shape[1]), jnp.float32)],
                            axis=1,
                        )
                    lined = piece if lined is None else lined + piece
                lined = shifted_left(lined, phase * STEP)[:, :span]
                total = lined if total is None else total + lined
            kernel = tmpl_ref[n, rows, :].astype(jnp.float32)
            mean = jnp.sum(kernel * kernel, axis=1, keepdims=True) / tmpl_len
            weight = 1.0 / (jnp.sqrt(mean + 1e-05) * tmpl_len)
            trace_ref[n, rows, :] = total * inverse_rms * weight

    lag = LAGS - 1 - lax.broadcasted_iota(jnp.int32, (LAGS, channels), 0)
    for n in range(count):
        pick = jnp.where(code_ref[n, 0:1, :channels] == lag, 1.0, 0.0).astype(jnp.bfloat16)
        trace = trace_ref[n]
        high = trace.astype(jnp.bfloat16)
        low = (trace - high.astype(jnp.float32)).astype(jnp.bfloat16)
        by_lag = jnp.dot(pick, high, preferred_element_type=jnp.float32)
        by_lag += jnp.dot(pick, low, preferred_element_type=jnp.float32)
        lined = pltpu.roll(by_lag, span - LAGS + 1, 1, stride=1, stride_axis=0)
        out_ref[n : n + 1, :] = jnp.sum(lined, axis=0, keepdims=True)[:, :slab_len]


def local(records, templates, channel_mask, lag_table):
    channels, slab_len = records.shape
    tmpl_len = templates.shape[3]
    second = templates.shape[2]
    tmpl_pad = up(tmpl_len, LANES)
    size = lax.axis_size("tm")
    count = size * templates.shape[1] * second
    span = up(slab_len + LAGS - 1, LANES)
    blocks = -(-tmpl_len // STEP)
    wide = blocks * STEP * ROWS
    tail = lax.ppermute(records, "tm", [(i + 1, i) for i in range(size - 1)])
    extended = jnp.concatenate([records, tail], axis=1)
    rows = jnp.transpose(templates, (1, 2, 0, 3)).reshape(-1, channels, tmpl_len)
    rows = jnp.pad(rows, ((0, 0), (0, 0), (0, tmpl_pad - tmpl_len)))
    code = jnp.where(channel_mask != 0, lag_table, -1)
    code = jnp.transpose(code, (1, 2, 0)).reshape(-1, 1, channels)
    rows = lax.all_gather(rows, "tm", axis=0, tiled=True)
    code = lax.all_gather(code, "tm", axis=0, tiled=True)
    out = pl.pallas_call(
        functools.partial(correlate, tmpl_len, count),
        out_shape=jax.ShapeDtypeStruct((count, slab_len), jnp.float32),
        in_specs=[pl.BlockSpec(memory_space=pltpu.VMEM)] * 3,
        out_specs=pl.BlockSpec(memory_space=pltpu.VMEM),
        scratch_shapes=[
            pltpu.VMEM((count, channels, wide), jnp.bfloat16),
            pltpu.VMEM((count, channels, span), jnp.float32),
            pltpu.VMEM((tmpl_pad, wide), jnp.bfloat16),
        ],
        compiler_params=pltpu.CompilerParams(vmem_limit_bytes=56 << 20),
    )(extended, rows, code)
    return out.reshape(count // second, second, slab_len)


def solution(mesh):
    return jax.shard_map(
        local,
        mesh=mesh,
        in_specs=(
            P(None, ("grp", "tm")),
            P(None, "tm", "tmpl", None),
            P(None, "tm", "tmpl"),
            P(None, "tm", "tmpl"),
        ),
        out_specs=P(None, "tmpl", ("grp", "tm")),
        check_vma=False,
    )
```

```python
import math

import jax
import jax.numpy as jnp
from jax import lax
from jax.experimental import pallas as pl
from jax.experimental.pallas import tpu as pltpu
from jax.sharding import PartitionSpec as P

LAGS = 64
LANES = 128
STEP = 32
ROWS = 16
GROUP = 8


def up(value, unit):
    return -(-value // unit) * unit


def shifted_left(values, count):
    width = values.shape[1]
    if count % width == 0:
        return values
    return pltpu.roll(values, width - count % width, 1)


def window_sum(values, length):
    total, done, power, span = None, 0, values, 1
    while True:
        if length & span:
            part = shifted_left(power, done)
            total = part if total is None else total + part
            done += span
        if span * 2 > length:
            return total
        power = power + shifted_left(power, span)
        span *= 2


def exchange(rec_ref, tmpl_ref, code_ref, tail_ref, slots_ref, codes_ref, sems):
    channels = rec_ref.shape[0]
    tm_size, grp_size = lax.axis_size("tm"), lax.axis_size("grp")
    me, part, col = lax.axis_index("tm"), lax.axis_index("grp"), lax.axis_index("tmpl")
    mate = col + 1 - 2 * (col % 2)
    share, half = channels // grp_size, channels // 2

    def there(axis, index):
        return {"device_id": {axis: index}, "device_id_type": pl.DeviceIdType.MESH}

    def copy(src, dst, name, index, where):
        send, recv = sems[name]
        return pltpu.make_async_remote_copy(
            src_ref=src, dst_ref=dst, send_sem=send.at[index], recv_sem=recv.at[index], **where
        )

    tm_peer = [(me + d) % tm_size for d in range(tm_size)]
    grp_peer = [(part + d) % grp_size for d in range(grp_size)]
    mine = pl.ds(pl.multiple_of(part * share, ROWS), share)
    piece = pl.ds(pl.multiple_of((col % 2) * half, ROWS), half)

    barrier = pltpu.get_barrier_semaphore()
    for d in range(1, tm_size):
        pl.semaphore_signal(barrier, inc=1, **there("tm", tm_peer[d]))
    for d in range(1, grp_size):
        pl.semaphore_signal(barrier, inc=1, **there("grp", grp_peer[d]))
    pl.semaphore_signal(barrier, inc=1, **there("tmpl", mate))

    rim = copy(rec_ref.at[piece], tail_ref.at[piece], "rim", 0, there("tm", jnp.maximum(me - 1, 0)))
    rim_on = copy(tail_ref.at[piece], tail_ref.at[piece], "rim", 1, there("tmpl", mate))
    sent = [
        copy(tmpl_ref.at[mine], slots_ref.at[d, mine], "tmpl", d, there("tm", tm_peer[d]))
        for d in range(1, tm_size)
    ]
    coded = [
        copy(code_ref, codes_ref.at[d], "code", d, there("tm", tm_peer[d])) for d in range(1, tm_size)
    ]
    passed = [
        [
            copy(
                slots_ref.at[d, mine],
                slots_ref.at[d, mine],
                "pass",
                d * grp_size + e,
                there("grp", grp_peer[e]),
            )
            for e in range(1, grp_size)
        ]
        for d in range(1, tm_size)
    ]

    def start():
        pl.semaphore_wait(barrier, tm_size + grp_size - 1)

        @pl.when(me > 0)
        def _():
            rim.start()

        for move in sent + coded:
            move.start()

    def land_rim():
        @pl.when(me < tm_size - 1)
        def _():
            rim.wait_recv()
            rim_on.start()
            rim_on.wait_recv()

        @pl.when(me == tm_size - 1)
        def _():
            tail_ref[...] = jnp.zeros_like(tail_ref)

    def pass_on():
        for move, onward in zip(sent, passed):
            move.wait_recv()
            for step in onward:
                step.start()

    def finish():
        for onward in passed:
            for step in onward:
                step.wait_recv()
        for move in coded:
            move.wait_recv()

    def drain():
        for move in sent + coded + [step for onward in passed for step in onward]:
            move.wait_send()

        @pl.when(me > 0)
        def _():
            rim.wait_send()

        @pl.when(me < tm_size - 1)
        def _():
            rim_on.wait_send()

    return start, land_rim, pass_on, finish, drain


def correlate(
    rec_ref,
    tmpl_ref,
    code_ref,
    out_ref,
    tail_ref,
    slots_ref,
    codes_ref,
    wide_ref,
    trace_ref,
    spread_ref,
    moved_ref,
    inverse_ref,
    *sem_refs,
):
    count, channels, tmpl_len = slots_ref.shape
    slab_len = rec_ref.shape[1]
    span = trace_ref.shape[2]
    blocks = -(-tmpl_len // STEP)
    wide = blocks * STEP * GROUP
    deep = STEP * GROUP
    reach = moved_ref.shape[2]
    per_tile = LANES // STEP
    batch = math.gcd(count, 4)
    names = ("rim", "tmpl", "code", "pass")
    sems = {name: sem_refs[2 * i : 2 * i + 2] for i, name in enumerate(names)}
    start, land_rim, pass_on, finish, drain = exchange(
        rec_ref, tmpl_ref, code_ref, tail_ref, slots_ref, codes_ref, sems
    )
    start()

    lane = lax.broadcasted_iota(jnp.int32, (tmpl_len, wide), 1)
    sample = lax.broadcasted_iota(jnp.int32, (tmpl_len, wide), 0)
    spread_ref[...] = jnp.where(lane // GROUP == sample, 1.0, 0.0).astype(jnp.bfloat16)
    slots_ref[0] = tmpl_ref[...]
    codes_ref[0] = code_ref[...]
    own = lax.broadcasted_iota(jnp.int32, (channels, wide), 1) % GROUP == (
        lax.broadcasted_iota(jnp.int32, (channels, wide), 0) % GROUP
    )

    def expand(n):
        kernel = slots_ref[n]
        widened = jnp.dot(kernel, spread_ref[...], preferred_element_type=jnp.float32)
        as_float = kernel.astype(jnp.float32)
        mean = jnp.sum(as_float * as_float, axis=1, keepdims=True) / tmpl_len
        weight = 1.0 / (jnp.sqrt(mean + 1e-05) * tmpl_len)
        wide_ref[n] = jnp.where(own, widened, 0.0)
        trace_ref[n] = jnp.broadcast_to(weight, (channels, span))

    expand(0)
    land_rim()

    @pl.loop(0, channels // ROWS)
    def _(pair):
        rows = pl.ds(pl.multiple_of(pair * ROWS, ROWS), ROWS)
        series = jnp.concatenate([rec_ref[rows, :], tail_ref[rows, :]], axis=1).astype(jnp.float32)
        energy = window_sum(series * series, tmpl_len)[:, :span]
        inverse_ref[rows, :] = lax.rsqrt(energy / tmpl_len + 1e-05)
        for side in range(ROWS // GROUP):
            part = series[side * GROUP : (side + 1) * GROUP]
            moved_ref[pair * (ROWS // GROUP) + side] = jnp.concatenate(
                [shifted_left(part, b)[:, :reach] for b in range(STEP)], axis=0
            ).astype(jnp.bfloat16)

    pass_on()
    finish()
    for n in range(1, count):
        expand(n)

    @pl.loop(0, count // batch)
    def _(turn):
        @pl.loop(0, channels // GROUP)
        def _(group):
            rows = pl.ds(pl.multiple_of(group * GROUP, GROUP), GROUP)
            left = jnp.concatenate(
                [
                    wide_ref[turn * batch + n, rows, a * deep : (a + 1) * deep]
                    for n in range(batch)
                    for a in range(blocks)
                ],
                axis=0,
            ).astype(jnp.bfloat16)
            partial = jnp.dot(left, moved_ref[group], preferred_element_type=jnp.float32)
            inverse_rms = inverse_ref[rows, :]
            for n in range(batch):
                total = None
                for phase in range(min(per_tile, blocks)):
                    lined = None
                    for a in range(phase, blocks, per_tile):
                        begin = (a - phase) * STEP
                        line = (n * blocks + a) * GROUP
                        piece = partial[line : line + GROUP, begin : begin + span + LANES]
                        if piece.shape[1] < span + LANES:
                            missing = span + LANES - piece.shape[1]
                            piece = jnp.concatenate(
                                [piece, jnp.zeros((GROUP, missing), jnp.float32)], axis=1
                            )
                        lined = piece if lined is None else lined + piece
                    lined = shifted_left(lined, phase * STEP)[:, :span]
                    total = lined if total is None else total + lined
                slot = turn * batch + n
                trace_ref[slot, rows, :] = total * inverse_rms * trace_ref[slot, rows, :]

    me = lax.axis_index("tm")
    lag = LAGS - 1 - lax.broadcasted_iota(jnp.int32, (LAGS, channels), 0)
    for n in range(count):
        pick = jnp.where(codes_ref[n] == lag, 1.0, 0.0).astype(jnp.bfloat16)
        trace = trace_ref[n]
        high = trace.astype(jnp.bfloat16)
        low = (trace - high.astype(jnp.float32)).astype(jnp.bfloat16)
        by_lag = jnp.dot(pick, high, preferred_element_type=jnp.float32)
        by_lag += jnp.dot(pick, low, preferred_element_type=jnp.float32)
        lined = pltpu.roll(by_lag, span - LAGS + 1, 1, stride=1, stride_axis=0)
        row = (me + count - n) % count
        out_ref[pl.ds(row, 1), :] = jnp.sum(lined, axis=0, keepdims=True)[:, :slab_len]
    drain()


def local(records, templates, channel_mask, lag_table):
    channels, slab_len = records.shape
    first, second, tmpl_len = templates.shape[1:]
    assert first == 1 and second == 1
    size, grp_size = lax.axis_size("tm"), lax.axis_size("grp")
    span = up(slab_len + LAGS - 1, LANES)
    blocks = -(-tmpl_len // STEP)
    wide = blocks * STEP * GROUP
    reach = up(slab_len + LAGS - 1 + (blocks - 1) * STEP, LANES)
    code = jnp.where(channel_mask != 0, lag_table, -1).reshape(1, channels)
    dma = pltpu.SemaphoreType.DMA
    out = pl.pallas_call(
        correlate,
        out_shape=jax.ShapeDtypeStruct((size, slab_len), jnp.float32),
        in_specs=[pl.BlockSpec(memory_space=pltpu.VMEM)] * 3,
        out_specs=pl.BlockSpec(memory_space=pltpu.VMEM),
        scratch_shapes=[
            pltpu.VMEM((channels, slab_len), jnp.bfloat16),
            pltpu.VMEM((size, channels, tmpl_len), jnp.bfloat16),
            pltpu.VMEM((size, 1, channels), jnp.int32),
            pltpu.VMEM((size, channels, wide), jnp.float32),
            pltpu.VMEM((size, channels, span), jnp.float32),
            pltpu.VMEM((tmpl_len, wide), jnp.bfloat16),
            pltpu.VMEM((channels // GROUP, STEP * GROUP, reach), jnp.bfloat16),
            pltpu.VMEM((channels, span), jnp.float32),
            dma((2,)),
            dma((2,)),
            dma((size,)),
            dma((size,)),
            dma((size,)),
            dma((size,)),
            dma((size * grp_size,)),
            dma((size * grp_size,)),
        ],
        compiler_params=pltpu.CompilerParams(
            vmem_limit_bytes=60 << 20, collective_id=0, has_side_effects=True
        ),
    )(records, templates.reshape(channels, tmpl_len), code)
    return out.reshape(size, 1, slab_len)


def solution(mesh):
    return jax.shard_map(
        local,
        mesh=mesh,
        in_specs=(
            P(None, ("grp", "tm")),
            P(None, "tm", "tmpl", None),
            P(None, "tm", "tmpl"),
            P(None, "tm", "tmpl"),
        ),
        out_specs=P(None, "tmpl", ("grp", "tm")),
        check_vma=False,
    )
```
